32 devices in a mesh: grp: 2 (over x), tm: 16 (over z, y, core).
Axes of the slice: x: 2, y: 2, z: 4, core: 2. Of those that a mesh axis runs over, the one named last changes fastest.
Arguments:
- block_input: bfloat16 [4, 16, 120, 384], P('grp', 'tm'), parts along dimension 0, may hold values from -6 to 6
- hidden_state: bfloat16 [4, 16, 120, 384], P('grp', 'tm'), parts along dimension 0, may hold values from -6 to 6
- norm_gain: float32 [384], replicated, may hold values from 0.5 to 1.5
- conv_weight: bfloat16 [3, 3, 3, 384, 384], replicated, may hold values from -0.0625 to 0.0625
- attn_gain: float32 [384], replicated, may hold values from 0.5 to 1.5
- qkv_weight: bfloat16 [384, 1152], replicated, may hold values from -4 to 4
- proj_weight: bfloat16 [384, 384], replicated, may hold values from -0.3125 to 0.3125
Outputs:
- block_output: bfloat16 [4, 16, 120, 384], P('grp', 'tm'), parts along dimension 0
The draws below stay inside these ranges and needn't reach their ends.
There are 2 independent parts, one for each index of `grp`. The reference program is written for one: setup_inputs(seed, part) draws one part's arguments, and reference() takes and returns one part's arrays. A program takes and returns all parts, laid end to end along the dimension named above; an argument that names none is the same for every part. Nothing has to cross between parts.
All inputs are finite; a program needn't handle non-finite values.
Results may differ from the reference program's by a relative error of at most 0.006.
Values may be sent and summed in bfloat16 or wider, within the bound.
A program may use at most 128 MiB of HBM per device.

```python
import jax
import jax.numpy as jnp
from jax import lax

C = 384
FRAMES = 2
COLS = 120
ROWS = 16


def draw_qkv_weight(key, part):
    first_key = jax.random.fold_in(key, 0)
    noise = jnp.clip(jax.random.normal(first_key, (C, 3 * C), jnp.float32), -4.0, 4.0) / jnp.sqrt(jnp.float32(C))
    return noise.astype(jnp.bfloat16)


def block_scale(own_key, shape, cuts, least, top_value):
    level = 1.0
    for dim, blocks in cuts:
        steps = jax.random.uniform(jax.random.fold_in(jax.random.fold_in(own_key, 6), dim), (blocks,), jnp.float32, least / len(cuts), top_value / len(cuts))
        level = level * jnp.repeat(jnp.exp(steps), shape[dim] // blocks).reshape((-1,) + (1,) * (len(shape) - 1 - dim))
    return level


def centred(rng, extent, scale, most, cuts=(), held_as=jnp.bfloat16):
    drawn = scale * jax.random.normal(rng, extent, jnp.float32)
    if cuts:
        drawn = drawn * block_scale(rng, extent, cuts, -0.22, 0.18)
    return jnp.clip(drawn, -most, most).astype(held_as)


def setup_inputs(seed: int = 0, part: int = 0) -> dict:
    arg_keys = jax.random.split(jax.random.key(seed), 8)
    part_splits = jax.random.split(jax.random.fold_in(arg_keys[7], part), 8)
    return {
        "block_input": centred(part_splits[0], (FRAMES, ROWS, COLS, C), 1.0, 6.0, ((1, 16),)),
        "hidden_state": centred(part_splits[1], (FRAMES, ROWS, COLS, C), 1.0, 6.0, ((1, 16),)),
        "norm_gain": jnp.clip(1.0 + 0.1 * jax.random.normal(arg_keys[2], (C,), jnp.float32), 0.5, 1.5),
        "conv_weight": centred(arg_keys[3], (3, 3, 3, C, C), (27 * C) ** -0.5, 0.0625),
        "attn_gain": jnp.clip(1.0 + 0.1 * jax.random.normal(arg_keys[4], (C,), jnp.float32), 0.5, 1.5),
        "qkv_weight": draw_qkv_weight(jax.random.fold_in(arg_keys[7], 71), part),
        "proj_weight": centred(arg_keys[6], (C, C), C ** -0.5, 0.3125),
    }


def rms_scale(values, gain):
    wide = values.astype(jnp.float32)
    return wide * lax.rsqrt(lax.optimization_barrier(jnp.mean(wide * wide, axis=-1, keepdims=True)) + 1e-06) * gain.astype(jnp.float32)

def conv_frame(padded, start, kernel):
    channels = padded.shape[-1]
    row_count = padded.shape[1] - 2
    col_count = padded.shape[2] - 2
    window = lax.dynamic_slice_in_dim(padded, start.astype(jnp.int32), 3, 0)
    pieces = [window[t_off, r_off:r_off + row_count, c_off:c_off + col_count, :] for t_off in range(3) for r_off in range(3) for c_off in range(3)]
    stacked = jnp.concatenate(pieces, axis=-1).reshape(-1, 27 * channels)
    result = jnp.dot(stacked, kernel.reshape(27 * channels, channels), preferred_element_type=jnp.float32)
    return result.reshape(row_count, col_count, channels)

def attend(normed_frame, mixed_frame, qkv_weight, proj_weight):
    channels = normed_frame.shape[-1]
    tokens = normed_frame.reshape(-1, channels)
    projected = jnp.dot(tokens, qkv_weight, preferred_element_type=jnp.float32).astype(jnp.bfloat16)
    queries = projected[:, :channels]
    key_part = projected[:, channels:2 * channels]
    value_part = projected[:, 2 * channels:]
    scores = jnp.dot(queries, key_part.T, preferred_element_type=jnp.float32) * channels ** (-0.5)
    scores = scores - lax.optimization_barrier(jnp.max(scores, axis=-1, keepdims=True))
    expo = jnp.exp(scores)
    weights = (expo / lax.optimization_barrier(jnp.sum(expo, axis=-1, keepdims=True))).astype(jnp.bfloat16)
    attended = jnp.dot(weights, value_part, preferred_element_type=jnp.float32).astype(jnp.bfloat16)
    result = mixed_frame.reshape(-1, channels).astype(jnp.float32) + jnp.dot(attended, proj_weight, preferred_element_type=jnp.float32)
    return result.astype(jnp.bfloat16).reshape(mixed_frame.shape)

def reference(block_input, hidden_state, norm_gain, conv_weight, attn_gain, qkv_weight, proj_weight):
    conv_in = jax.nn.silu(rms_scale(hidden_state, norm_gain)).astype(jnp.bfloat16)
    padded = jnp.pad(conv_in, ((2, 0), (1, 1), (1, 1), (0, 0)))
    frame_ids = jnp.arange(block_input.shape[0], dtype=jnp.int32)
    conv_out = lax.map(lambda start: conv_frame(padded, start, conv_weight), frame_ids)
    mixed = (block_input.astype(jnp.float32) + conv_out).astype(jnp.bfloat16)
    normed = rms_scale(mixed, attn_gain).astype(jnp.bfloat16)
    return lax.map(lambda pair: attend(pair[0], pair[1], qkv_weight, proj_weight), (normed, mixed))
```

```python
import functools

import jax
import jax.numpy as jnp
from jax import lax
from jax.experimental import pallas as pl
from jax.experimental.pallas import tpu as pltpu
from jax.sharding import PartitionSpec as P

CORES = 2


def halo_kernel(n, x_ref, before_ref, after_ref, sems, recv):
    me = lax.axis_index("tm")
    rows = x_ref.shape[1]
    barrier = pltpu.get_barrier_semaphore()

    @pl.when(me > 0)
    def _():
        pl.semaphore_signal(barrier, inc=1, device_id={"tm": me - 1})

    @pl.when(me < n - 1)
    def _():
        pl.semaphore_signal(barrier, inc=1, device_id={"tm": me + 1})

    inner = jnp.logical_and(me > 0, me < n - 1)
    pl.semaphore_wait(barrier, jnp.where(inner, 2, 1))

    def to_next():
        return pltpu.make_async_remote_copy(
            x_ref.at[:, rows - 1], before_ref, sems.at[0], recv.at[0], device_id={"tm": me + 1}
        )

    def to_previous():
        return pltpu.make_async_remote_copy(
            x_ref.at[:, 0], after_ref, sems.at[1], recv.at[1], device_id={"tm": me - 1}
        )

    @pl.when(me < n - 1)
    def _():
        to_next().start()

    @pl.when(me > 0)
    def _():
        to_previous().start()

    @pl.when(me == 0)
    def _():
        before_ref[...] = jnp.zeros_like(before_ref)

    @pl.when(me == n - 1)
    def _():
        after_ref[...] = jnp.zeros_like(after_ref)

    @pl.when(me < n - 1)
    def _():
        to_next().wait_send()
        to_previous().wait_recv()

    @pl.when(me > 0)
    def _():
        to_previous().wait_send()
        to_next().wait_recv()


def halo(x, n):
    frames, _, cols, channels = x.shape
    edge = jax.ShapeDtypeStruct((frames, cols, channels), x.dtype)
    vmem = pl.BlockSpec(memory_space=pltpu.VMEM)
    return pl.pallas_call(
        functools.partial(halo_kernel, n),
        out_shape=(edge, edge),
        in_specs=[vmem],
        out_specs=(vmem, vmem),
        scratch_shapes=[pltpu.SemaphoreType.DMA((2,)), pltpu.SemaphoreType.DMA((2,))],
        compiler_params=pltpu.CompilerParams(collective_id=0, has_side_effects=True),
    )(x)


def gather_kernel(zn, yn, x_ref, out_ref, local_sem, up, down, across, twin, recv):
    frames = x_ref.shape[0]
    me = lax.axis_index("tm")
    c = lax.rem(me, CORES)
    y = lax.rem(me // CORES, yn)
    z = me // (CORES * yn)

    def index(zz, yy, cc):
        return (zz * yn + yy) * CORES + cc

    below, above = index(z - 1, y, c), index(z + 1, y, c)
    sibling, opposite = index(z, y, 1 - c), index(z, yn - 1 - y, c)
    has_below, has_above = z > 0, z < zn - 1

    barrier = pltpu.get_barrier_semaphore()
    pl.semaphore_signal(barrier, inc=1, device_id={"tm": sibling})
    if yn > 1:
        pl.semaphore_signal(barrier, inc=1, device_id={"tm": opposite})

    @pl.when(has_below)
    def _():
        pl.semaphore_signal(barrier, inc=1, device_id={"tm": below})

    @pl.when(has_above)
    def _():
        pl.semaphore_signal(barrier, inc=1, device_id={"tm": above})

    inner = jnp.logical_and(has_below, has_above)
    pl.semaphore_wait(barrier, yn + (jnp.where(inner, 2, 1) if zn > 1 else 0))

    def copy(zz, yy, cc, f, send, target, own=False):
        owner = index(zz, yy, cc)
        return pltpu.make_async_remote_copy(
            x_ref.at[f] if own else out_ref.at[f, owner],
            out_ref.at[f, owner],
            send,
            recv.at[owner, f],
            device_id={"tm": target},
        )

    def up_copy(zz, f, own=False):
        return copy(zz, y, c, f, up.at[zz, f], above, own)

    def down_copy(zz, f, own=False):
        return copy(zz, y, c, f, down.at[zz, f], below, own)

    def across_copy(zz, f, own=False):
        return copy(zz, y, c, f, across.at[zz, f], opposite, own)

    def twin_copy(zz, yy, f, own=False):
        return copy(zz, yy, c, f, twin.at[zz, yy, f], sibling, own)

    def arrived(zz, yy, cc, f):
        copy(zz, yy, cc, f, up.at[0, 0], sibling).wait_recv()

    def own_copy(f):
        return pltpu.make_async_copy(x_ref.at[f], out_ref.at[f, me], local_sem.at[f])

    for f in range(frames):

        @pl.when(has_above)
        def _():
            up_copy(z, f, True).start()

        @pl.when(has_below)
        def _():
            down_copy(z, f, True).start()

        if yn > 1:
            across_copy(z, f, True).start()
        twin_copy(z, y, f, True).start()
        own_copy(f).start()

    def from_across(zz, f):
        arrived(zz, yn - 1 - y, c, f)
        twin_copy(zz, yn - 1 - y, f).start()

    def step(d, part):
        for f in range(frames):

            @pl.when(z - d >= 0)
            def _():
                part(z - d, f, True)

            @pl.when(z + d < zn)
            def _():
                part(z + d, f, False)

    def along(zz, f, from_below):
        arrived(zz, y, c, f)
        if from_below:

            @pl.when(has_above)
            def _():
                up_copy(zz, f).start()
        else:

            @pl.when(has_below)
            def _():
                down_copy(zz, f).start()

        if yn > 1:
            across_copy(zz, f).start()
        twin_copy(zz, y, f).start()

    def crossed(zz, f, from_below):
        from_across(zz, f)

    for d in range(1, zn):
        step(d, along)
        if yn > 1:
            if d == 1:
                for f in range(frames):
                    from_across(z, f)
            else:
                step(d - 1, crossed)
    if yn > 1:
        if zn == 1:
            for f in range(frames):
                from_across(z, f)
        else:
            step(zn - 1, crossed)

    for zz in range(zn):
        for f in range(frames):
            for yy in range(yn):
                arrived(zz, yy, 1 - c, f)
                twin_copy(zz, yy, f).wait_send()
            if yn > 1:
                across_copy(zz, f).wait_send()

            @pl.when(jnp.logical_and(has_above, zz <= z))
            def _():
                up_copy(zz, f).wait_send()

            @pl.when(jnp.logical_and(has_below, zz >= z))
            def _():
                down_copy(zz, f).wait_send()

    for f in range(frames):
        own_copy(f).wait()


def gather(x, n):
    frames, rows, channels = x.shape
    yn = 2 if n % (2 * CORES) == 0 else 1
    zn = n // (CORES * yn)
    vmem = pl.BlockSpec(memory_space=pltpu.VMEM)
    dma = pltpu.SemaphoreType.DMA
    return pl.pallas_call(
        functools.partial(gather_kernel, zn, yn),
        out_shape=jax.ShapeDtypeStruct((frames, n, rows, channels), x.dtype),
        in_specs=[vmem],
        out_specs=vmem,
        scratch_shapes=[
            dma((frames,)),
            dma((zn, frames)),
            dma((zn, frames)),
            dma((zn, frames)),
            dma((zn, yn, frames)),
            dma((n, frames)),
        ],
        compiler_params=pltpu.CompilerParams(
            collective_id=1, has_side_effects=True, vmem_limit_bytes=48 * 2**20
        ),
    )(x)


def rms_scale(values, gain):
    wide = values.astype(jnp.float32)
    return wide * lax.rsqrt(jnp.mean(wide * wide, axis=-1, keepdims=True) + 1e-06) * gain


def causal_conv(padded, kernel):
    channels = padded.shape[-1]
    frames = padded.shape[0] - 2
    row_count = padded.shape[1] - 2
    col_count = padded.shape[2] - 2
    pieces = [
        padded[t_off : t_off + frames, r_off : r_off + row_count, c_off : c_off + col_count, :]
        for t_off in range(3)
        for r_off in range(3)
        for c_off in range(3)
    ]
    stacked = jnp.concatenate(pieces, axis=-1).reshape(-1, 27 * channels)
    result = jnp.dot(
        stacked, kernel.reshape(27 * channels, channels), preferred_element_type=jnp.float32
    )
    return result.reshape(frames, row_count, col_count, channels)


def attend(queries, normed, mixed_frame, qkv_weight, proj_weight):
    channels = queries.shape[-1]
    key_value = jnp.dot(
        normed, qkv_weight[:, channels:], preferred_element_type=jnp.float32
    ).astype(jnp.bfloat16)
    key_part = key_value[:, :channels]
    value_part = key_value[:, channels:]
    scores = jnp.dot(queries, key_part.T, preferred_element_type=jnp.float32) * channels ** (-0.5)
    scores = scores - jnp.max(scores, axis=-1, keepdims=True)
    expo = jnp.exp(scores)
    weights = (expo / jnp.sum(expo, axis=-1, keepdims=True)).astype(jnp.bfloat16)
    attended = jnp.dot(weights, value_part, preferred_element_type=jnp.float32).astype(jnp.bfloat16)
    result = mixed_frame.astype(jnp.float32) + jnp.dot(
        attended, proj_weight, preferred_element_type=jnp.float32
    )
    return result.astype(jnp.bfloat16)


def body(block_input, hidden_state, norm_gain, conv_weight, attn_gain, qkv_weight, proj_weight):
    n = lax.axis_size("tm")
    me = lax.axis_index("tm")
    frames, rows, cols, channels = block_input.shape
    before, after = halo(hidden_state, n)
    padded = jnp.concatenate([before[:, None], hidden_state, after[:, None]], axis=1)
    conv_in = jax.nn.silu(rms_scale(padded, norm_gain)).astype(jnp.bfloat16)
    padded = jnp.pad(conv_in, ((2, 0), (0, 0), (1, 1), (0, 0)))
    conv_out = causal_conv(padded, conv_weight)
    mixed = (block_input.astype(jnp.float32) + conv_out).astype(jnp.bfloat16)
    normed = rms_scale(mixed, attn_gain).astype(jnp.bfloat16)
    local = rows * cols
    normed = normed.reshape(frames, local, channels)
    mixed = mixed.reshape(frames, local, channels)
    queries = jnp.dot(
        normed, qkv_weight[:, :channels], preferred_element_type=jnp.float32
    ).astype(jnp.bfloat16)
    whole = gather(normed, n).reshape(frames, n * local, channels)
    outs = [
        attend(queries[f], whole[f], mixed[f], qkv_weight, proj_weight) for f in range(frames)
    ]
    return jnp.stack(outs).reshape(block_input.shape)


def solution(mesh):
    return jax.shard_map(
        body,
        mesh=mesh,
        in_specs=(P("grp", "tm", None, None), P("grp", "tm", None, None), P(), P(), P(), P(), P()),
        out_specs=P("grp", "tm", None, None),
        check_vma=False,
    )
```

```python
import functools

import jax
import jax.numpy as jnp
from jax import lax
from jax.experimental import pallas as pl
from jax.experimental.pallas import tpu as pltpu
from jax.sharding import PartitionSpec as P

CORES = 2


def halo_kernel(n, x_ref, before_ref, after_ref, sems, recv):
    me = lax.axis_index("tm")
    rows = x_ref.shape[1]
    barrier = pltpu.get_barrier_semaphore()

    @pl.when(me > 0)
    def _():
        pl.semaphore_signal(barrier, inc=1, device_id={"tm": me - 1})

    @pl.when(me < n - 1)
    def _():
        pl.semaphore_signal(barrier, inc=1, device_id={"tm": me + 1})

    inner = jnp.logical_and(me > 0, me < n - 1)
    pl.semaphore_wait(barrier, jnp.where(inner, 2, 1))

    def to_next():
        return pltpu.make_async_remote_copy(
            x_ref.at[:, rows - 1], before_ref, sems.at[0], recv.at[0], device_id={"tm": me + 1}
        )

    def to_previous():
        return pltpu.make_async_remote_copy(
            x_ref.at[:, 0], after_ref, sems.at[1], recv.at[1], device_id={"tm": me - 1}
        )

    @pl.when(me < n - 1)
    def _():
        to_next().start()

    @pl.when(me > 0)
    def _():
        to_previous().start()

    @pl.when(me == 0)
    def _():
        before_ref[...] = jnp.zeros_like(before_ref)

    @pl.when(me == n - 1)
    def _():
        after_ref[...] = jnp.zeros_like(after_ref)

    @pl.when(me < n - 1)
    def _():
        to_next().wait_send()
        to_previous().wait_recv()

    @pl.when(me > 0)
    def _():
        to_previous().wait_send()
        to_next().wait_recv()


def halo(x, n):
    frames, _, cols, channels = x.shape
    edge = jax.ShapeDtypeStruct((frames, cols, channels), x.dtype)
    vmem = pl.BlockSpec(memory_space=pltpu.VMEM)
    return pl.pallas_call(
        functools.partial(halo_kernel, n),
        out_shape=(edge, edge),
        in_specs=[vmem],
        out_specs=(vmem, vmem),
        scratch_shapes=[pltpu.SemaphoreType.DMA((2,)), pltpu.SemaphoreType.DMA((2,))],
        compiler_params=pltpu.CompilerParams(collective_id=0, has_side_effects=True),
    )(x)


def gather_kernel(zn, yn, x_ref, out_ref, local_sem, up, down, across, twin, recv):
    frames = x_ref.shape[0]
    me = lax.axis_index("tm")
    c = lax.rem(me, CORES)
    y = lax.rem(me // CORES, yn)
    z = me // (CORES * yn)

    def index(zz, yy, cc):
        return (zz * yn + yy) * CORES + cc

    below, above = index(z - 1, y, c), index(z + 1, y, c)
    sibling, opposite = index(z, y, 1 - c), index(z, yn - 1 - y, c)
    has_below, has_above = z > 0, z < zn - 1

    barrier = pltpu.get_barrier_semaphore()
    pl.semaphore_signal(barrier, inc=1, device_id={"tm": sibling})
    if yn > 1:
        pl.semaphore_signal(barrier, inc=1, device_id={"tm": opposite})

    @pl.when(has_below)
    def _():
        pl.semaphore_signal(barrier, inc=1, device_id={"tm": below})

    @pl.when(has_above)
    def _():
        pl.semaphore_signal(barrier, inc=1, device_id={"tm": above})

    inner = jnp.logical_and(has_below, has_above)
    pl.semaphore_wait(barrier, yn + (jnp.where(inner, 2, 1) if zn > 1 else 0))

    def copy(zz, yy, cc, f, send, target, own=False):
        owner = index(zz, yy, cc)
        return pltpu.make_async_remote_copy(
            x_ref.at[f] if own else out_ref.at[f, owner],
            out_ref.at[f, owner],
            send,
            recv.at[owner, f],
            device_id={"tm": target},
        )

    def up_copy(zz, f, own=False):
        return copy(zz, y, c, f, up.at[zz, f], above, own)

    def down_copy(zz, f, own=False):
        return copy(zz, y, c, f, down.at[zz, f], below, own)

    def across_copy(zz, f, own=False):
        return copy(zz, y, c, f, across.at[zz, f], opposite, own)

    def twin_copy(zz, yy, f, own=False):
        return copy(zz, yy, c, f, twin.at[zz, yy, f], sibling, own)

    def arrived(zz, yy, cc, f):
        copy(zz, yy, cc, f, up.at[0, 0], sibling).wait_recv()

    def own_copy(f):
        return pltpu.make_async_copy(x_ref.at[f], out_ref.at[f, me], local_sem.at[f])

    for f in range(frames):

        @pl.when(has_above)
        def _():
            up_copy(z, f, True).start()

        @pl.when(has_below)
        def _():
            down_copy(z, f, True).start()

        if yn > 1:
            across_copy(z, f, True).start()
        twin_copy(z, y, f, True).start()
        own_copy(f).start()

    def from_across(zz, f):
        arrived(zz, yn - 1 - y, c, f)
        twin_copy(zz, yn - 1 - y, f).start()

    def step(d, part):
        for f in range(frames):

            @pl.when(z - d >= 0)
            def _():
                part(z - d, f, True)

            @pl.when(z + d < zn)
            def _():
                part(z + d, f, False)

    def along(zz, f, from_below):
        arrived(zz, y, c, f)
        if from_below:

            @pl.when(has_above)
            def _():
                up_copy(zz, f).start()
        else:

            @pl.when(has_below)
            def _():
                down_copy(zz, f).start()

        if yn > 1:
            across_copy(zz, f).start()
        twin_copy(zz, y, f).start()

    def crossed(zz, f, from_below):
        from_across(zz, f)

    for d in range(1, zn):
        step(d, along)
        if yn > 1:
            if d == 1:
                for f in range(frames):
                    from_across(z, f)
            else:
                step(d - 1, crossed)
    if yn > 1:
        if zn == 1:
            for f in range(frames):
                from_across(z, f)
        else:
            step(zn - 1, crossed)

    for zz in range(zn):
        for f in range(frames):
            for yy in range(yn):
                arrived(zz, yy, 1 - c, f)
                twin_copy(zz, yy, f).wait_send()
            if yn > 1:
                across_copy(zz, f).wait_send()

            @pl.when(jnp.logical_and(has_above, zz <= z))
            def _():
                up_copy(zz, f).wait_send()

            @pl.when(jnp.logical_and(has_below, zz >= z))
            def _():
                down_copy(zz, f).wait_send()

    for f in range(frames):
        own_copy(f).wait()


def gather(x, n):
    frames, rows, channels = x.shape
    yn = 2 if n % (2 * CORES) == 0 else 1
    zn = n // (CORES * yn)
    vmem = pl.BlockSpec(memory_space=pltpu.VMEM)
    dma = pltpu.SemaphoreType.DMA
    return pl.pallas_call(
        functools.partial(gather_kernel, zn, yn),
        out_shape=jax.ShapeDtypeStruct((frames, n, rows, channels), x.dtype),
        in_specs=[vmem],
        out_specs=vmem,
        scratch_shapes=[
            dma((frames,)),
            dma((zn, frames)),
            dma((zn, frames)),
            dma((zn, frames)),
            dma((zn, yn, frames)),
            dma((n, frames)),
        ],
        compiler_params=pltpu.CompilerParams(
            collective_id=1, has_side_effects=True, vmem_limit_bytes=48 * 2**20
        ),
    )(x)


def rms_scale(values, gain):
    wide = values.astype(jnp.float32)
    return wide * lax.rsqrt(jnp.mean(wide * wide, axis=-1, keepdims=True) + 1e-06) * gain


def causal_conv(padded, kernel):
    channels = padded.shape[-1]
    frames = padded.shape[0] - 2
    row_count = padded.shape[1] - 2
    col_count = padded.shape[2] - 2
    pieces = [
        padded[t_off : t_off + frames, r_off : r_off + row_count, c_off : c_off + col_count, :]
        for t_off in range(3)
        for r_off in range(3)
        for c_off in range(3)
    ]
    stacked = jnp.concatenate(pieces, axis=-1).reshape(-1, 27 * channels)
    result = jnp.dot(
        stacked, kernel.reshape(27 * channels, channels), preferred_element_type=jnp.float32
    )
    return result.reshape(frames, row_count, col_count, channels)


def halves(values):
    high = lax.reduce_precision(values, 8, 7)
    return high.astype(jnp.bfloat16), (values - high).astype(jnp.bfloat16)


def dot(a, b):
    return jnp.dot(a, b, preferred_element_type=jnp.float32)


def attend(queries, normed, mixed_frame, value_weight, proj_weight):
    local, channels = mixed_frame.shape
    both = lax.dot_general(
        queries, normed, (((1,), (1,)), ((), ())), preferred_element_type=jnp.float32
    )
    scores = (both[:local] + both[local:]) * channels ** (-0.5)
    scores = scores - jnp.max(scores, axis=-1, keepdims=True)
    expo = jnp.exp(scores)
    weights = (expo / jnp.sum(expo, axis=-1, keepdims=True)).astype(jnp.bfloat16)
    high, low = halves(dot(weights, normed))
    attended = (dot(high, value_weight) + dot(low, value_weight)).astype(jnp.bfloat16)
    result = mixed_frame.astype(jnp.float32) + dot(attended, proj_weight)
    return result.astype(jnp.bfloat16)


def body(block_input, hidden_state, norm_gain, conv_weight, attn_gain, qkv_weight, proj_weight):
    n = lax.axis_size("tm")
    me = lax.axis_index("tm")
    frames, rows, cols, channels = block_input.shape
    before, after = halo(hidden_state, n)
    padded = jnp.concatenate([before[:, None], hidden_state, after[:, None]], axis=1)
    conv_in = jax.nn.silu(rms_scale(padded, norm_gain)).astype(jnp.bfloat16)
    padded = jnp.pad(conv_in, ((2, 0), (0, 0), (1, 1), (0, 0)))
    conv_out = causal_conv(padded, conv_weight)
    mixed = (block_input.astype(jnp.float32) + conv_out).astype(jnp.bfloat16)
    normed = rms_scale(mixed, attn_gain).astype(jnp.bfloat16)
    local = rows * cols
    normed = normed.reshape(frames, local, channels)
    mixed = mixed.reshape(frames, local, channels)
    queries = jnp.dot(
        normed, qkv_weight[:, :channels], preferred_element_type=jnp.float32
    ).astype(jnp.bfloat16)
    key_weight = qkv_weight[:, channels : 2 * channels]
    value_weight = qkv_weight[:, 2 * channels :]
    high, low = halves(
        lax.dot_general(
            queries, key_weight, (((2,), (1,)), ((), ())), preferred_element_type=jnp.float32
        )
    )
    queries = jnp.concatenate([high, low], axis=1)
    whole = gather(normed, n).reshape(frames, n * local, channels)
    outs = [
        attend(queries[f], whole[f], mixed[f], value_weight, proj_weight) for f in range(frames)
    ]
    return jnp.stack(outs).reshape(block_input.shape)


def solution(mesh):
    return jax.shard_map(
        body,
        mesh=mesh,
        in_specs=(P("grp", "tm", None, None), P("grp", "tm", None, None), P(), P(), P(), P(), P()),
        out_specs=P("grp", "tm", None, None),
        check_vma=False,
    )
```

```python
import functools

import jax
import jax.numpy as jnp
from jax import lax
from jax.experimental import pallas as pl
from jax.experimental.pallas import tpu as pltpu
from jax.sharding import PartitionSpec as P

CORES = 2


def halo_kernel(n, x_ref, weight_ref, before_ref, after_ref, held_ref, sems, recv, weight_sem):
    weight_copy = pltpu.make_async_copy(weight_ref, held_ref, weight_sem)
    weight_copy.start()
    me = lax.axis_index("tm")
    rows = x_ref.shape[1]
    barrier = pltpu.get_barrier_semaphore()

    @pl.when(me > 0)
    def _():
        pl.semaphore_signal(barrier, inc=1, device_id={"tm": me - 1})

    @pl.when(me < n - 1)
    def _():
        pl.semaphore_signal(barrier, inc=1, device_id={"tm": me + 1})

    inner = jnp.logical_and(me > 0, me < n - 1)
    pl.semaphore_wait(barrier, jnp.where(inner, 2, 1))

    def to_next():
        return pltpu.make_async_remote_copy(
            x_ref.at[:, rows - 1], before_ref, sems.at[0], recv.at[0], device_id={"tm": me + 1}
        )

    def to_previous():
        return pltpu.make_async_remote_copy(
            x_ref.at[:, 0], after_ref, sems.at[1], recv.at[1], device_id={"tm": me - 1}
        )

    @pl.when(me < n - 1)
    def _():
        to_next().start()

    @pl.when(me > 0)
    def _():
        to_previous().start()

    @pl.when(me == 0)
    def _():
        before_ref[...] = jnp.zeros_like(before_ref)

    @pl.when(me == n - 1)
    def _():
        after_ref[...] = jnp.zeros_like(after_ref)

    @pl.when(me < n - 1)
    def _():
        to_next().wait_send()
        to_previous().wait_recv()

    @pl.when(me > 0)
    def _():
        to_previous().wait_send()
        to_next().wait_recv()

    weight_copy.wait()


def halo(x, weight, n):
    frames, _, cols, channels = x.shape
    edge = jax.ShapeDtypeStruct((frames, cols, channels), x.dtype)
    vmem = pl.BlockSpec(memory_space=pltpu.VMEM)
    return pl.pallas_call(
        functools.partial(halo_kernel, n),
        out_shape=(edge, edge, jax.ShapeDtypeStruct(weight.shape, weight.dtype)),
        in_specs=[pl.BlockSpec(memory_space=pltpu.HBM)] * 2,
        out_specs=(vmem, vmem, vmem),
        scratch_shapes=[
            pltpu.SemaphoreType.DMA((2,)),
            pltpu.SemaphoreType.DMA((2,)),
            pltpu.SemaphoreType.DMA,
        ],
        compiler_params=pltpu.CompilerParams(collective_id=0, has_side_effects=True, vmem_limit_bytes=weight.size * 2 + 4 * 2**20),
    )(x, weight)


def gather_kernel(zn, yn, x_ref, out_ref, local_sem, up, down, across, twin, recv):
    splits = x_ref.shape[1]
    pieces = x_ref.shape[0] * splits
    me = lax.axis_index("tm")
    c = lax.rem(me, CORES)
    y = lax.rem(me // CORES, yn)
    z = me // (CORES * yn)

    def index(zz, yy, cc):
        return (zz * yn + yy) * CORES + cc

    below, above = index(z - 1, y, c), index(z + 1, y, c)
    sibling, opposite = index(z, y, 1 - c), index(z, yn - 1 - y, c)
    has_below, has_above = z > 0, z < zn - 1

    barrier = pltpu.get_barrier_semaphore()
    pl.semaphore_signal(barrier, inc=1, device_id={"tm": sibling})
    if yn > 1:
        pl.semaphore_signal(barrier, inc=1, device_id={"tm": opposite})

    @pl.when(has_below)
    def _():
        pl.semaphore_signal(barrier, inc=1, device_id={"tm": below})

    @pl.when(has_above)
    def _():
        pl.semaphore_signal(barrier, inc=1, device_id={"tm": above})

    inner = jnp.logical_and(has_below, has_above)
    pl.semaphore_wait(barrier, yn + (jnp.where(inner, 2, 1) if zn > 1 else 0))

    def landing(owner, f):
        return out_ref.at[f // splits, owner, f % splits]

    def copy(zz, yy, cc, f, send, target, own=False):
        owner = index(zz, yy, cc)
        return pltpu.make_async_remote_copy(
            x_ref.at[f // splits, f % splits] if own else landing(owner, f),
            landing(owner, f),
            send,
            recv.at[owner, f],
            device_id={"tm": target},
        )

    def up_copy(zz, f, own=False):
        return copy(zz, y, c, f, up.at[zz, f], above, own)

    def down_copy(zz, f, own=False):
        return copy(zz, y, c, f, down.at[zz, f], below, own)

    def across_copy(zz, f, own=False):
        return copy(zz, y, c, f, across.at[zz, f], opposite, own)

    def twin_copy(zz, yy, f, own=False):
        return copy(zz, yy, c, f, twin.at[zz, yy, f], sibling, own)

    def arrived(zz, yy, cc, f):
        copy(zz, yy, cc, f, up.at[0, 0], sibling).wait_recv()

    def own_copy(f):
        return pltpu.make_async_copy(
            x_ref.at[f // splits, f % splits], landing(me, f), local_sem.at[f]
        )

    for f in range(pieces):

        @pl.when(has_above)
        def _():
            up_copy(z, f, True).start()

        @pl.when(has_below)
        def _():
            down_copy(z, f, True).start()

        if yn > 1:
            across_copy(z, f, True).start()
        twin_copy(z, y, f, True).start()
        own_copy(f).start()

    def from_across(zz, f):
        arrived(zz, yn - 1 - y, c, f)
        twin_copy(zz, yn - 1 - y, f).start()

    def step(d, part):
        for f in range(pieces):

            @pl.when(z - d >= 0)
            def _():
                part(z - d, f, True)

            @pl.when(z + d < zn)
            def _():
                part(z + d, f, False)

    def along(zz, f, from_below):
        arrived(zz, y, c, f)
        if from_below:

            @pl.when(has_above)
            def _():
                up_copy(zz, f).start()
        else:

            @pl.when(has_below)
            def _():
                down_copy(zz, f).start()

        if yn > 1:
            across_copy(zz, f).start()
        twin_copy(zz, y, f).start()

    def crossed(zz, f, from_below):
        from_across(zz, f)

    for d in range(1, zn):
        step(d, along)
        if yn > 1:
            if d == 1:
                for f in range(pieces):
                    from_across(z, f)
            else:
                step(d - 1, crossed)
    if yn > 1:
        if zn == 1:
            for f in range(pieces):
                from_across(z, f)
        else:
            step(zn - 1, crossed)

    for zz in range(zn):
        for f in range(pieces):
            for yy in range(yn):
                arrived(zz, yy, 1 - c, f)
                twin_copy(zz, yy, f).wait_send()
            if yn > 1:
                across_copy(zz, f).wait_send()

            @pl.when(jnp.logical_and(has_above, zz <= z))
            def _():
                up_copy(zz, f).wait_send()

            @pl.when(jnp.logical_and(has_below, zz >= z))
            def _():
                down_copy(zz, f).wait_send()

    for f in range(pieces):
        own_copy(f).wait()


def gather(x, n):
    frames, rows, channels = x.shape
    yn = 2 if n % (2 * CORES) == 0 else 1
    zn = n // (CORES * yn)
    splits = 3 if rows % 24 == 0 else 1
    pieces = frames * splits
    x = x.reshape(frames, splits, rows // splits, channels)
    vmem = pl.BlockSpec(memory_space=pltpu.VMEM)
    dma = pltpu.SemaphoreType.DMA
    return pl.pallas_call(
        functools.partial(gather_kernel, zn, yn),
        out_shape=jax.ShapeDtypeStruct((frames, n, *x.shape[1:]), x.dtype),
        in_specs=[vmem],
        out_specs=vmem,
        scratch_shapes=[
            dma((pieces,)),
            dma((zn, pieces)),
            dma((zn, pieces)),
            dma((zn, pieces)),
            dma((zn, yn, pieces)),
            dma((n, pieces)),
        ],
        compiler_params=pltpu.CompilerParams(
            collective_id=1, has_side_effects=True, vmem_limit_bytes=(n + 2) * 2 * x.size * 2 + 2**20
        ),
    )(x)


def rms_scale(values, gain):
    wide = values.astype(jnp.float32)
    return wide * lax.rsqrt(jnp.mean(wide * wide, axis=-1, keepdims=True) + 1e-06) * gain


def causal_conv(padded, kernel):
    channels = padded.shape[-1]
    frames = padded.shape[0] - 2
    row_count = padded.shape[1] - 2
    col_count = padded.shape[2] - 2
    pieces = [
        padded[t_off : t_off + frames, r_off : r_off + row_count, c_off : c_off + col_count, :]
        for t_off in range(3)
        for r_off in range(3)
        for c_off in range(3)
    ]
    stacked = jnp.concatenate(pieces, axis=-1).reshape(-1, 27 * channels)
    result = jnp.dot(
        stacked, kernel, preferred_element_type=jnp.float32
    )
    return result.reshape(frames, row_count, col_count, channels)


def halves(values):
    high = lax.reduce_precision(values, 8, 7)
    return high.astype(jnp.bfloat16), (values - high).astype(jnp.bfloat16)


def dot(a, b):
    return jnp.dot(a, b, preferred_element_type=jnp.float32)


def attend(queries, normed, mixed_frame, value_weight, proj_weight):
    local, channels = mixed_frame.shape
    both = lax.dot_general(
        queries, normed, (((1,), (1,)), ((), ())), preferred_element_type=jnp.float32
    )
    scores = (both[:local] + both[local:]) * channels ** (-0.5)
    scores = scores - jnp.max(scores, axis=-1, keepdims=True)
    expo = jnp.exp(scores)
    weights = (expo / jnp.sum(expo, axis=-1, keepdims=True)).astype(jnp.bfloat16)
    high, low = halves(dot(weights, normed))
    attended = (dot(high, value_weight) + dot(low, value_weight)).astype(jnp.bfloat16)
    result = mixed_frame.astype(jnp.float32) + dot(attended, proj_weight)
    return result.astype(jnp.bfloat16)


def body(block_input, hidden_state, norm_gain, conv_weight, attn_gain, qkv_weight, proj_weight):
    n = lax.axis_size("tm")
    me = lax.axis_index("tm")
    frames, rows, cols, channels = block_input.shape
    before, after, conv_weight = halo(
        hidden_state, conv_weight.reshape(-1, conv_weight.shape[-1]), n
    )
    padded = jnp.concatenate([before[:, None], hidden_state, after[:, None]], axis=1)
    conv_in = jax.nn.silu(rms_scale(padded, norm_gain)).astype(jnp.bfloat16)
    padded = jnp.pad(conv_in, ((2, 0), (0, 0), (1, 1), (0, 0)))
    conv_out = causal_conv(padded, conv_weight)
    mixed = (block_input.astype(jnp.float32) + conv_out).astype(jnp.bfloat16)
    normed = rms_scale(mixed, attn_gain).astype(jnp.bfloat16)
    local = rows * cols
    normed = normed.reshape(frames, local, channels)
    mixed = mixed.reshape(frames, local, channels)
    queries = jnp.dot(
        normed, qkv_weight[:, :channels], preferred_element_type=jnp.float32
    ).astype(jnp.bfloat16)
    key_weight = qkv_weight[:, channels : 2 * channels]
    value_weight = qkv_weight[:, 2 * channels :]
    high, low = halves(
        lax.dot_general(
            queries, key_weight, (((2,), (1,)), ((), ())), preferred_element_type=jnp.float32
        )
    )
    queries = jnp.concatenate([high, low], axis=1)
    whole = gather(normed, n).reshape(frames, n * local, channels)
    outs = [
        attend(queries[f], whole[f], mixed[f], value_weight, proj_weight) for f in range(frames)
    ]
    return jnp.stack(outs).reshape(block_input.shape)


def solution(mesh):
    return jax.shard_map(
        body,
        mesh=mesh,
        in_specs=(P("grp", "tm", None, None), P("grp", "tm", None, None), P(), P(), P(), P(), P()),
        out_specs=P("grp", "tm", None, None),
        check_vma=False,
    )
```
